32 devices in a mesh: section: 4 (over y, x), row: 8 (over z, core).
Axes of the slice: x: 2, y: 2, z: 4, core: 2. Of those that a mesh axis runs over, the one named last changes fastest.
Arguments:
- object_slices: float32 [4, 2, 1024, 1024], P('section', None, 'row'), may hold values from -5 to 5
- probe_spec: float32 [2, 1024, 1024], P(None, 'row'), may hold values from -5 to 5
- offsets: int32 [2, 2], replicated, may hold values from 0 to 1023
- measured: float32 [2, 1024, 1024], P(None, 'row'), may hold values from 0.2 to 3
Outputs:
- object_grad: float32 [4, 2, 1024, 1024], P('section', None, 'row')
The draws below stay inside these ranges and needn't reach their ends.
All inputs are finite; a program needn't handle non-finite values.
Results may differ from the reference program's by a relative error of at most 0.0003.
Values sent between devices are 32-bit elements; how exact they have to be, the bound alone decides.
A program may use at most 128 MiB of HBM per device.

```python
import math
import jax
import jax.numpy as jnp

N = 1024
WAVES = 2
SLICES = 4


def plant(drawn, rng, smallest, top_value):
    spot = [jax.random.randint(jax.random.fold_in(rng, axis), (), 0, length) for axis, length in enumerate(drawn.shape)]
    longest = drawn.shape.index(max(drawn.shape))
    next_to = spot[:longest] + [(spot[longest] + 1) % drawn.shape[longest]] + spot[longest + 1:]
    return drawn.at[tuple(spot)].set(smallest).at[tuple(next_to)].set(top_value)


def level_of(rng, dims, pieces, low, top_value):
    level = 1.0
    for dim, blocks in pieces:
        draws = jax.random.uniform(jax.random.fold_in(jax.random.fold_in(rng, 6), dim), (blocks,), jnp.float32, low / len(pieces), top_value / len(pieces))
        level = level * jnp.repeat(jnp.exp(draws), dims[dim] // blocks).reshape((-1,) + (1,) * (len(dims) - 1 - dim))
    return level


def scatter_about(key, shape, scale, most, split=(), kind=jnp.bfloat16):
    values = scale * jax.random.normal(key, shape, jnp.float32)
    if split:
        values = values * level_of(key, shape, split, -0.22, 0.18)
    return jnp.clip(values, -most, most).astype(kind)


def setup_inputs(seed: int = 0) -> dict:
    keys = jax.random.split(jax.random.key(seed), 5)
    return {
        "object_slices": scatter_about(keys[0], (SLICES, 2, N, N), 0.7, 5.0, ((0, 4), (2, 8)), jnp.float32),
        "probe_spec": scatter_about(keys[1], (2, N, N), 0.7, 5.0, ((1, 8),), jnp.float32),
        "offsets": plant(jax.random.randint(keys[2], (WAVES, 2), 0, N), jax.random.fold_in(keys[2], 1), 0, N - 1).astype(jnp.int32),
        "measured": jnp.clip(jnp.exp(math.log(3.0) - 2.7080502 * jax.random.uniform(keys[3], (WAVES, N, N), jnp.float32) ** level_of(keys[3], (WAVES, N, N), ((1, 8),), -0.2, 0.2)), 0.2, 3.0),
    }


fresnel_coef = 0.37

def reorder(stored):
    lead = stored.shape[:-2]
    moved = stored.reshape(lead + (2, N // 2, N))
    moved = jnp.swapaxes(moved, -3, -2).reshape(lead + (N, N))
    moved = moved.reshape(lead + (N, 2, N // 2))
    return jnp.swapaxes(moved, -2, -1).reshape(lead + (N, N))

def reference(object_slices, probe_spec, offsets, measured):
    freq = jnp.arange(N, dtype=jnp.int32)
    signed = jnp.where(freq < N // 2, freq, freq - N)
    square = signed * signed
    phase = -math.pi * fresnel_coef / N * (square[:, None] + square[None, :]).astype(jnp.float32)
    propagator = jnp.cos(phase) + 1j * jnp.sin(phase)
    spectrum = (probe_spec[0] + 1j * probe_spec[1]).T
    targets = jnp.swapaxes(measured, 1, 2)

    def loss_of(real_part, imag_part):
        field = reorder(real_part) + 1j * reorder(imag_part)
        total = jnp.zeros((), jnp.float32)
        for wave in range(WAVES):
            turns = (freq[:, None] * offsets[wave, 0] + freq[None, :] * offsets[wave, 1]) % N
            angle = 2.0 * math.pi / N * turns.astype(jnp.float32)
            ramp = jnp.cos(angle) - 1j * jnp.sin(angle)
            wavefield = jnp.fft.ifft2(spectrum * ramp, norm='ortho')
            for layer in range(SLICES):
                outgoing = jnp.fft.fft2(field[layer] * wavefield, norm='ortho')
                if layer < SLICES - 1:
                    wavefield = jnp.fft.ifft2(propagator * outgoing, norm='ortho')
            power = jnp.real(outgoing) ** 2 + jnp.imag(outgoing) ** 2
            total = total + 0.125 * jnp.sum((power - targets[wave]) ** 2)
        return total
    grads = jax.grad(loss_of, argnums=(0, 1))(object_slices[:, 0], object_slices[:, 1])
    return jnp.stack(grads, axis=1)
```

```python
import math

import jax
import jax.numpy as jnp
import numpy as np
from jax import lax
from jax.experimental import pallas as pl
from jax.experimental.pallas import tpu as pltpu
from jax.sharding import PartitionSpec as P

fresnel_coef = 0.37
highest = lax.Precision.HIGHEST


def complex_mul(left, right):
    return jnp.stack(
        [left[0] * right[0] - left[1] * right[1], left[0] * right[1] + left[1] * right[0]]
    )


def conj_mul(left, right):
    return jnp.stack(
        [left[0] * right[0] + left[1] * right[1], left[1] * right[0] - left[0] * right[1]]
    )


def combine_parts(result, half_len, direction):
    first = result[..., :half_len]
    second = result[..., half_len:]
    return jnp.stack([first[0] + direction * second[1], first[1] - direction * second[0]])


def small_dft(stacked, tables, direction):
    half_len = tables[0].shape[0]
    both_tables = jnp.concatenate([tables[0], tables[1]], axis=1)
    flat = stacked.reshape(-1, half_len)
    result = jnp.dot(flat, both_tables, precision=highest)
    result = result.reshape(stacked.shape[:-1] + (2 * half_len,))
    return combine_parts(result, half_len, direction)


def forward_pass(field, tables):
    half_len = tables[0].shape[0]
    halves = field.reshape(field.shape[0], field.shape[1], field.shape[2], 2, half_len)
    spectra = small_dft(halves, tables, 1.0)
    even_part = spectra[:, :, :, 0]
    turned = complex_mul(spectra[:, :, :, 1], jnp.stack([tables[2], -tables[3]]))
    joined = jnp.stack([even_part + turned, even_part - turned], axis=3)
    return joined.reshape(joined.shape[0], joined.shape[1], joined.shape[2], 2 * half_len)


def inverse_pass(field, tables):
    half_len = tables[0].shape[0]
    first_half = field[:, :, :, :half_len]
    second_half = field[:, :, :, half_len:]
    twiddle = jnp.stack([tables[2], tables[3]])
    halves = jnp.stack(
        [first_half + second_half, complex_mul(first_half - second_half, twiddle)], axis=3
    )
    spectra = small_dft(halves, tables, -1.0)
    return spectra.reshape(spectra.shape[0], spectra.shape[1], spectra.shape[2], 2 * half_len)


def forward_columns(field, tables):
    half_len = tables[0].shape[0]
    lines = field.shape[3]
    both_tables = jnp.concatenate([tables[0], tables[1]], axis=1)
    halves = field.reshape(field.shape[0], field.shape[1], 2, half_len, lines)
    result = jnp.einsum("cwajl,jk->cwalk", halves, both_tables, precision=highest)
    spectra = combine_parts(result, half_len, 1.0)
    even_part = spectra[:, :, 0]
    turned = complex_mul(spectra[:, :, 1], jnp.stack([tables[2], -tables[3]]))
    joined = jnp.stack([even_part + turned, even_part - turned], axis=3)
    return joined.reshape(joined.shape[0], joined.shape[1], lines, 2 * half_len)


def inverse_columns(field, tables):
    half_len = tables[0].shape[0]
    lines = field.shape[3]
    both_tables = jnp.concatenate([tables[0], tables[1]], axis=1)
    first_half = field[:, :, :half_len]
    second_half = field[:, :, half_len:]
    twiddle = jnp.stack([tables[2][:, None], tables[3][:, None]])
    halves = jnp.stack(
        [first_half + second_half, complex_mul(first_half - second_half, twiddle)], axis=2
    )
    result = jnp.einsum("cwajl,jk->cwlak", halves, both_tables, precision=highest)
    spectra = combine_parts(result, half_len, -1.0)
    return spectra.reshape(spectra.shape[0], spectra.shape[1], lines, 2 * half_len)


def transform_forward(field, tables):
    partial_out = forward_pass(field, tables)

    def finish(piece):
        return forward_columns(piece, tables)

    return finish(lax.all_to_all(partial_out, "row", split_axis=3, concat_axis=2, tiled=True))


def transform_inverse(field, tables):
    partial_out = inverse_pass(field, tables)

    def finish(piece):
        return inverse_columns(piece, tables)

    return finish(lax.all_to_all(partial_out, "row", split_axis=3, concat_axis=2, tiled=True))


def section_forward(spectrum, multiplier, slab_obj, propagator, tables):
    wavefield = transform_inverse(complex_mul(spectrum, multiplier), tables)
    kept = []
    outgoing = wavefield
    for layer in range(slab_obj.shape[0]):
        kept.append(wavefield)
        outgoing = transform_forward(complex_mul(slab_obj[layer][:, None], wavefield), tables)
        if layer + 1 < slab_obj.shape[0]:
            wavefield = transform_inverse(complex_mul(outgoing, propagator), tables)
    return (outgoing, jnp.stack(kept))


def section_backward(adjoint, kept, multiplier, slab_obj, propagator, tables):
    layer_total = slab_obj.shape[0]
    grads = [None] * layer_total
    for layer in reversed(range(layer_total)):
        wave_adj = transform_inverse(adjoint, tables)
        grads[layer] = jnp.sum(conj_mul(wave_adj, kept[layer]), axis=1)
        field_adj = conj_mul(wave_adj, slab_obj[layer][:, None])
        backward_spec = transform_forward(field_adj, tables)
        if layer > 0:
            adjoint = conj_mul(backward_spec, propagator)
        else:
            adjoint = conj_mul(backward_spec, multiplier)
    return (adjoint, jnp.stack(grads))


def loss_adjoint(outgoing, target):
    power = outgoing[0] * outgoing[0] + outgoing[1] * outgoing[1]
    return 0.5 * (power - target)[None] * outgoing


def shards(object_slices, probe_spec, offsets, measured):
    line_count = object_slices.shape[2]
    width = object_slices.shape[3]
    half_len = width // 2
    wave_count = offsets.shape[0]
    section_count = lax.axis_size("section")
    section_pos = lax.axis_index("section")
    row_pos = lax.axis_index("row")
    index = jnp.arange(half_len, dtype=jnp.int32)
    product = index[:, None] * index[None, :] % half_len
    angle = 2.0 * math.pi / half_len * product.astype(jnp.float32)
    scale = 1.0 / math.sqrt(width)
    twid_angle = 2.0 * math.pi / width * index.astype(jnp.float32)
    tables = (
        jnp.cos(angle) * scale,
        jnp.sin(angle) * scale,
        jnp.cos(twid_angle),
        jnp.sin(twid_angle),
    )
    column_freq = row_pos * line_count + jnp.arange(line_count, dtype=jnp.int32)
    row_freq = jnp.arange(width, dtype=jnp.int32)
    column_signed = jnp.where(column_freq < half_len, column_freq, column_freq - width)
    row_signed = jnp.where(row_freq < half_len, row_freq, row_freq - width)
    square_sum = (
        column_signed[:, None] * column_signed[:, None] + row_signed[None, :] * row_signed[None, :]
    )
    phase = -math.pi * fresnel_coef / width * square_sum.astype(jnp.float32)
    propagator = jnp.stack([jnp.cos(phase), jnp.sin(phase)])[:, None]
    turns = (
        row_freq[None, None, :] * offsets[:, 0][:, None, None]
        + column_freq[None, :, None] * offsets[:, 1][:, None, None]
    ) % width
    ramp_angle = 2.0 * math.pi / width * turns.astype(jnp.float32)
    ramps = jnp.stack([jnp.cos(ramp_angle), -jnp.sin(ramp_angle)])
    start_spec = probe_spec[:, None]
    all_obj = lax.all_gather(object_slices, "section", axis=0, tiled=True)
    wave_pick = section_pos % wave_count
    ramp_pick = lax.dynamic_slice_in_dim(ramps, wave_pick, 1, axis=1)
    outgoing, kept = section_forward(start_spec, ramp_pick, all_obj, propagator, tables)
    target = lax.dynamic_slice_in_dim(measured, wave_pick, 1, axis=0)
    unused, grads = section_backward(
        loss_adjoint(outgoing, target), kept, ramp_pick, all_obj, propagator, tables
    )
    summed = lax.psum_scatter(grads, "section", scatter_dimension=0, tiled=True)
    return summed * (wave_count / section_count)


def split_table(table):
    both = np.concatenate([table.real, table.imag], axis=-1).astype(np.float32)
    high = both.astype(jnp.bfloat16)
    low = (both - high.astype(np.float32)).astype(jnp.bfloat16)
    return high, low


def fused_tables(width):
    half, quarter = width // 2, width // 4
    freq = np.arange(width)
    signed = np.where(freq < half, freq, freq - width).astype(np.float64)
    response = np.exp(-1j * np.pi * fresnel_coef / width * signed * signed)
    place = np.arange(quarter)
    place = np.where(place < quarter // 2, 2 * place, 2 * (place - quarter // 2) + 1)
    gap = place[None, :] - place[:, None]
    circ = []
    for turn in range(4):
        line = np.zeros(width, np.complex128)
        line[turn::4] = response[turn::4]
        kernel = np.fft.ifft(line)
        circ.append(kernel[gap % width])
    index = np.arange(half)
    even = np.exp(-2j * np.pi * (2 * index[:, None] * index[None, :] % width) / width)
    odd = np.exp(-2j * np.pi * ((2 * index[:, None] + 1) * index[None, :] % width) / width)
    scale = 1.0 / math.sqrt(width)
    dft = np.stack([even, odd, odd.T]) * scale
    return split_table(np.stack(circ)) + split_table(dft)


def dot_split(left, high, low):
    left_high = left.astype(jnp.bfloat16)
    left_low = (left - left_high.astype(jnp.float32)).astype(jnp.bfloat16)
    out = jnp.dot(left_low, high, preferred_element_type=jnp.float32)
    out += jnp.dot(left_high, low, preferred_element_type=jnp.float32)
    return out + jnp.dot(left_high, high, preferred_element_type=jnp.float32)


def complex_dot(left, high, low):
    out = dot_split(left, high, low)
    lines, width = out.shape[0] // 2, out.shape[1] // 2
    real = out[:lines, :width] - out[lines:, width:]
    imag = out[:lines, width:] + out[lines:, :width]
    return jnp.concatenate([real, imag], axis=0)


def times_i(value):
    lines = value.shape[0] // 2
    return jnp.concatenate([-value[lines:], value[:lines]], axis=0)


def fused_kernel(
    dims, obj_ref, spec_ref, meas_ref, ramp_y, ramp_x, circ_h, circ_l, dft_h, dft_l, out_ref,
    state, send, recv, spec_in, meas_out, meas_in, obj_out, obj_row, obj_col, kept, grad_out,
    grad_row, grad_col, send_sem, recv_sem, spec_sem, meas_sem, obj_send, obj_sem, grad_send,
    grad_sem,
):
    sections, rows, waves, layers, width = dims
    wave_rows = rows // waves
    group = sections * wave_rows
    lines = width // group
    shard = width // rows
    per = shard // lines
    half, chunk = width // 2, width // 8
    sec = lax.axis_index("section")
    row = lax.axis_index("row")
    wave = row // wave_rows
    mine = (row % wave_rows) * sections + sec
    total = sections * rows
    me = sec * rows + row

    def place(of_wave, member):
        return member % sections, of_wave * wave_rows + member // sections

    def push(src, dst, sent, got, to_sec, to_row):
        home = jnp.logical_and(to_sec == sec, to_row == row)

        @pl.when(home)
        def _():
            pltpu.make_async_copy(src, dst, got).start()

        @pl.when(jnp.logical_not(home))
        def _():
            pltpu.make_async_remote_copy(
                src_ref=src, dst_ref=dst, send_sem=sent, recv_sem=got,
                device_id=(to_sec, to_row), device_id_type=pl.DeviceIdType.MESH,
            ).start()

    def settle(src, sent, to_sec, to_row):
        @pl.when(jnp.logical_not(jnp.logical_and(to_sec == sec, to_row == row)))
        def _():
            pltpu.make_async_copy(src, src, sent).wait()

    barrier = pltpu.get_barrier_semaphore()

    def greet(step, carry):
        other = (me + step) % total
        pl.semaphore_signal(
            barrier, inc=1, device_id=(other // rows, other % rows),
            device_id_type=pl.DeviceIdType.MESH,
        )
        return carry

    lax.fori_loop(1, total, greet, 0)
    pl.semaphore_wait(barrier, total - 1)

    spec_wave = sec // per
    spec_part = sec % per
    spec_to = place(spec_wave, row * per + spec_part)
    spec_src = spec_ref.at[:, pl.ds(pl.multiple_of(spec_part * lines, lines), lines)]
    push(spec_src, spec_in, spec_sem.at[0], spec_sem.at[1], *spec_to)

    def obj_row_push(layer, act):
        for part in range(per):
            for of_wave in range(waves):
                src = obj_ref.at[:, pl.ds(part * lines, lines)]
                to = place(of_wave, row * per + part)
                if act:
                    push(src, obj_row.at[layer // 2], obj_send.at[0], obj_sem.at[layer], *to)
                else:
                    settle(src, obj_send.at[0], *to)

    def obj_col_push(layer, act):
        def step(count, carry):
            member = count // waves
            of_wave = count % waves
            to = place(of_wave, member)
            src = obj_out.at[member]
            if act:
                push(src, obj_col.at[layer // 2, row], obj_send.at[0], obj_sem.at[layer], *to)
            else:
                settle(src, obj_send.at[0], *to)
            return carry

        lax.fori_loop(0, group * waves, step, 0)

    def transpose_obj():
        for block in range(width // shard):
            for part in range(2):
                turned = obj_ref[part, :, block * shard:(block + 1) * shard].T
                for piece in range(per):
                    obj_out[block * per + piece, :, part * shard:(part + 1) * shard] = (
                        turned[piece * lines:(piece + 1) * lines]
                    )

    for layer in range(layers):
        @pl.when(sec == layer)
        def _(layer=layer):
            if layer % 2 == 0:
                obj_row_push(layer, True)
            else:
                transpose_obj()
                obj_col_push(layer, True)

    span = width // sections
    for of_wave in range(waves):
        piece = meas_ref[of_wave, :, pl.ds(pl.multiple_of(sec * span, span), span)].T
        for part in range(group // sections):
            meas_out[of_wave, part] = piece[part * lines:(part + 1) * lines]

    def meas_push(act):
        for of_wave in range(waves):
            for part in range(group // sections):
                to = place(of_wave, sec * (group // sections) + part)
                src = meas_out.at[of_wave, part]
                if act:
                    push(src, meas_in.at[row], meas_sem.at[0], meas_sem.at[1], *to)
                else:
                    settle(src, meas_sem.at[0], *to)

    meas_push(True)

    def circ_pass():
        x = [
            jnp.concatenate(
                [state[:, b * chunk:(b + 1) * chunk],
                 state[:, half + b * chunk:half + (b + 1) * chunk]], axis=1)
            for b in range(4)
        ]
        sum_a, dif_a = x[0] + x[2], x[0] - x[2]
        sum_b, dif_b = x[1] + x[3], times_i(x[1] - x[3])
        folded = (sum_a + sum_b, dif_a - dif_b, sum_a - sum_b, dif_a + dif_b)
        y = [complex_dot(folded[t], circ_h[t], circ_l[t]) for t in range(4)]
        sum_a, dif_a = y[0] + y[2], y[0] - y[2]
        sum_b, dif_b = y[1] + y[3], times_i(y[1] - y[3])
        for b, value in enumerate((sum_a + sum_b, dif_a + dif_b, sum_a - sum_b, dif_a - dif_b)):
            state[:, b * chunk:(b + 1) * chunk] = value[:, :chunk]
            state[:, half + b * chunk:half + (b + 1) * chunk] = value[:, chunk:]

    def to_freq():
        even = complex_dot(state[:, :half], dft_h[0], dft_l[0])
        odd = complex_dot(state[:, half:], dft_h[1], dft_l[1])
        state[:, :half] = even + odd
        state[:, half:] = even - odd

    def from_freq():
        first, second = state[:, :half], state[:, half:]
        state[:, :half] = complex_dot(first + second, dft_h[0], dft_l[0])
        state[:, half:] = complex_dot(first - second, dft_h[2], dft_l[2])

    pair = 2 * lines

    def exchange(step):
        for block in range(width // pair):
            turned = state[:, block * pair:(block + 1) * pair].T
            send[step, 2 * block] = turned[:lines]
            send[step, 2 * block + 1] = turned[lines:]

        def start(count, carry):
            other = (mine + count) % group
            to_sec, to_row = place(wave, other)
            pltpu.make_async_remote_copy(
                src_ref=send.at[step, other], dst_ref=recv.at[step, mine],
                send_sem=send_sem.at[step], recv_sem=recv_sem.at[step],
                device_id=(to_sec, to_row), device_id_type=pl.DeviceIdType.MESH,
            ).start()
            return carry

        lax.fori_loop(1, group, start, 0)
        recv[step, mine] = send[step, mine]
        arrived = recv.at[step, pl.ds(0, group - 1)]
        pltpu.make_async_copy(arrived, arrived, recv_sem.at[step]).wait()
        low = lax.broadcasted_iota(jnp.int32, (lines, pair), 1) < lines
        for block in range(width // pair):
            one, two = recv[step, 2 * block], recv[step, 2 * block + 1]
            cols = slice(block * pair, (block + 1) * pair)
            state[:lines, cols] = jnp.where(low, one, pltpu.roll(two, lines, 1))
            state[lines:, cols] = jnp.where(low, pltpu.roll(one, lines, 1), two)

    def wait_object(layer):
        if layer % 2 == 0:
            buf = obj_row.at[layer // 2]
        else:
            buf = obj_col.at[layer // 2]
        pltpu.make_async_copy(buf, buf, obj_sem.at[layer]).wait()

    def times_object(layer):
        for r in range(rows):
            cols = slice(r * shard, (r + 1) * shard)
            if layer % 2 == 0:
                o_re, o_im = obj_row[layer // 2, 0, :, cols], obj_row[layer // 2, 1, :, cols]
            else:
                o_re = obj_col[layer // 2, r, :, :shard]
                o_im = obj_col[layer // 2, r, :, shard:]
            re, im = state[:lines, cols], state[lines:, cols]
            state[:lines, cols] = o_re * re - o_im * im
            state[lines:, cols] = o_re * im + o_im * re

    def grad_push(layer, act):
        if layer % 2 == 0:
            to = (layer, mine // per)
            dst = grad_row.at[wave, mine % per]
            src = grad_out.at[layer]
            if act:
                push(src, dst, grad_send.at[layer], grad_sem.at[0], *to)
            else:
                settle(src, grad_send.at[layer], *to)
        else:
            for r in range(rows):
                src = grad_out.at[layer, :, :, pl.ds(r * shard, shard)]
                dst = grad_col.at[wave, mine, :, :, :]
                if act:
                    push(src, dst, grad_send.at[layer], grad_sem.at[0], layer, r)
                else:
                    settle(src, grad_send.at[layer], layer, r)

    def gradient(layer):
        for r in range(rows):
            cols = slice(r * shard, (r + 1) * shard)
            re, im = state[:lines, cols], state[lines:, cols]
            k_re, k_im = kept[layer, :lines, cols], kept[layer, lines:, cols]
            grad_out[layer, 0, :, cols] = re * k_re - im * k_im
            grad_out[layer, 1, :, cols] = -(re * k_im + im * k_re)
        grad_push(layer, True)

    pltpu.make_async_copy(spec_in, spec_in, spec_sem.at[1]).wait()
    y_re, y_im = ramp_y[0], ramp_y[1]
    x_re, x_im = ramp_x[0], ramp_x[1]
    turn_re = x_re * y_re - x_im * y_im
    turn_im = x_re * y_im + x_im * y_re
    p_re, p_im = spec_in[0], spec_in[1]
    state[:lines] = p_re * turn_re + p_im * turn_im
    state[lines:] = p_re * turn_im - p_im * turn_re
    from_freq()
    exchange(0)
    from_freq()
    state[lines:] = -state[lines:]
    for layer in range(layers):
        kept[layer] = state[...]
        wait_object(layer)
        times_object(layer)
        if layer + 1 < layers:
            circ_pass()
            exchange(1 + layer)
            circ_pass()
    to_freq()
    exchange(layers)
    to_freq()
    pltpu.make_async_copy(meas_in, meas_in, meas_sem.at[1]).wait()
    for r in range(rows):
        cols = slice(r * shard, (r + 1) * shard)
        re, im = state[:lines, cols], state[lines:, cols]
        weight = 0.5 * (re * re + im * im - meas_in[r])
        state[:lines, cols] = weight * re
        state[lines:, cols] = -(weight * im)
    from_freq()
    exchange(layers + 1)
    from_freq()
    for layer in reversed(range(layers)):
        gradient(layer)
        if layer > 0:
            times_object(layer)
            circ_pass()
            exchange(layers + 1 + layers - layer)
            circ_pass()

    settle(spec_src, spec_sem.at[0], *spec_to)
    meas_push(False)
    for layer in range(layers):
        grad_push(layer, False)

        @pl.when(sec == layer)
        def _(layer=layer):
            if layer % 2 == 0:
                obj_row_push(layer, False)
            else:
                obj_col_push(layer, False)
    for step in range(2 * layers + 1):
        gone = send.at[step, pl.ds(0, group - 1)]
        pltpu.make_async_copy(gone, gone, send_sem.at[step]).wait()

    @pl.when(sec % 2 == 0)
    def _():
        pltpu.make_async_copy(grad_row, grad_row, grad_sem.at[0]).wait()
        for part in range(per):
            value = grad_row[0, part]
            for of_wave in range(1, waves):
                value = value + grad_row[of_wave, part]
            out_ref[:, part * lines:(part + 1) * lines] = value

    @pl.when(sec % 2 == 1)
    def _():
        pltpu.make_async_copy(grad_col, grad_col, grad_sem.at[0]).wait()
        for block in range(width // pair):
            for part in range(2):
                pieces = []
                for member in (2 * block, 2 * block + 1):
                    value = grad_col[0, member, part]
                    for of_wave in range(1, waves):
                        value = value + grad_col[of_wave, member, part]
                    pieces.append(value)
                out_ref[part, :, block * pair:(block + 1) * pair] = jnp.concatenate(pieces, axis=0).T


def fused_shards(object_slices, probe_spec, offsets, measured):
    sections, rows = lax.axis_size("section"), lax.axis_size("row")
    width = object_slices.shape[3]
    waves = offsets.shape[0]
    layers = sections * object_slices.shape[0]
    dims = (sections, rows, waves, layers, width)
    wave_rows = rows // waves
    group = sections * wave_rows
    lines = width // group
    shard = width // rows
    row = lax.axis_index("row")
    mine = (row % wave_rows) * sections + lax.axis_index("section")
    shift = lax.dynamic_index_in_dim(offsets, row // wave_rows, 0, keepdims=False)
    unit = 2.0 * math.pi / width
    turn_y = unit * (jnp.arange(width, dtype=jnp.int32) * shift[0] % width).astype(jnp.float32)
    line = mine * lines + jnp.arange(lines, dtype=jnp.int32)
    turn_x = unit * (line * shift[1] % width).astype(jnp.float32)
    ramp_y = jnp.stack([jnp.cos(turn_y), jnp.sin(turn_y)])[:, None, :]
    ramp_x = jnp.stack([jnp.cos(turn_x), jnp.sin(turn_x)])[:, :, None]
    tables = [jnp.asarray(t) for t in fused_tables(width)]
    steps = 2 * layers + 1
    f32 = jnp.float32
    vmem = pl.BlockSpec(memory_space=pltpu.VMEM)
    even, odd = (layers + 1) // 2, layers // 2
    dma = pltpu.SemaphoreType.DMA
    result = pl.pallas_call(
        lambda *refs: fused_kernel(dims, *refs),
        out_shape=jax.ShapeDtypeStruct((2, shard, width), f32),
        in_specs=[vmem] * 9,
        out_specs=vmem,
        scratch_shapes=[
            pltpu.VMEM((2 * lines, width), f32),
            pltpu.VMEM((steps, group, lines, 2 * lines), f32),
            pltpu.VMEM((steps, group, lines, 2 * lines), f32),
            pltpu.VMEM((2, lines, width), f32),
            pltpu.VMEM((waves, group // sections, lines, shard), f32),
            pltpu.VMEM((rows, lines, shard), f32),
            pltpu.VMEM((group, lines, 2 * shard), f32),
            pltpu.VMEM((even, 2, lines, width), f32),
            pltpu.VMEM((odd, rows, lines, 2 * shard), f32),
            pltpu.VMEM((layers, 2 * lines, width), f32),
            pltpu.VMEM((layers, 2, lines, width), f32),
            pltpu.VMEM((waves, shard // lines, 2, lines, width), f32),
            pltpu.VMEM((waves, group, 2, lines, shard), f32),
            dma((steps,)),
            dma((steps,)),
            dma((2,)),
            dma((2,)),
            dma((1,)),
            dma((layers,)),
            dma((layers,)),
            dma((1,)),
        ],
        compiler_params=pltpu.CompilerParams(
            collective_id=0, has_side_effects=True, vmem_limit_bytes=60 * 1024 * 1024
        ),
    )(object_slices[0], probe_spec, measured, ramp_y, ramp_x, *tables)
    return result[None]


def fused_fits(sections, rows, waves, layers, width):
    if rows % waves or layers != sections or layers % 2:
        return False
    group = sections * rows // waves
    if width % group or width % rows or group % sections:
        return False
    lines, shard = width // group, width // rows
    if 2 * lines != 128 or shard != 2 * lines or width % 1024:
        return False
    return sections == waves * (shard // lines)


def solution(mesh):
    placed = (P("section", None, "row", None), P(None, "row", None), P(), P(None, "row", None))

    def build(body):
        return jax.shard_map(
            body,
            mesh=mesh,
            in_specs=placed,
            out_specs=P("section", None, "row", None),
            check_vma=False,
        )

    def run(object_slices, probe_spec, offsets, measured):
        fits = fused_fits(
            mesh.shape["section"], mesh.shape["row"], offsets.shape[0],
            object_slices.shape[0], object_slices.shape[3],
        )
        body = fused_shards if fits else shards
        return build(body)(object_slices, probe_spec, offsets, measured)

    return run
```

```python
import math

import jax
import jax.numpy as jnp
import numpy as np
from jax import lax
from jax.experimental import pallas as pl
from jax.experimental.pallas import tpu as pltpu
from jax.sharding import PartitionSpec as P

fresnel_coef = 0.37
highest = lax.Precision.HIGHEST


def complex_mul(left, right):
    return jnp.stack(
        [left[0] * right[0] - left[1] * right[1], left[0] * right[1] + left[1] * right[0]]
    )


def conj_mul(left, right):
    return jnp.stack(
        [left[0] * right[0] + left[1] * right[1], left[1] * right[0] - left[0] * right[1]]
    )


def combine_parts(result, half_len, direction):
    first = result[..., :half_len]
    second = result[..., half_len:]
    return jnp.stack([first[0] + direction * second[1], first[1] - direction * second[0]])


def small_dft(stacked, tables, direction):
    half_len = tables[0].shape[0]
    both_tables = jnp.concatenate([tables[0], tables[1]], axis=1)
    flat = stacked.reshape(-1, half_len)
    result = jnp.dot(flat, both_tables, precision=highest)
    result = result.reshape(stacked.shape[:-1] + (2 * half_len,))
    return combine_parts(result, half_len, direction)


def forward_pass(field, tables):
    half_len = tables[0].shape[0]
    halves = field.reshape(field.shape[0], field.shape[1], field.shape[2], 2, half_len)
    spectra = small_dft(halves, tables, 1.0)
    even_part = spectra[:, :, :, 0]
    turned = complex_mul(spectra[:, :, :, 1], jnp.stack([tables[2], -tables[3]]))
    joined = jnp.stack([even_part + turned, even_part - turned], axis=3)
    return joined.reshape(joined.shape[0], joined.shape[1], joined.shape[2], 2 * half_len)


def inverse_pass(field, tables):
    half_len = tables[0].shape[0]
    first_half = field[:, :, :, :half_len]
    second_half = field[:, :, :, half_len:]
    twiddle = jnp.stack([tables[2], tables[3]])
    halves = jnp.stack(
        [first_half + second_half, complex_mul(first_half - second_half, twiddle)], axis=3
    )
    spectra = small_dft(halves, tables, -1.0)
    return spectra.reshape(spectra.shape[0], spectra.shape[1], spectra.shape[2], 2 * half_len)


def forward_columns(field, tables):
    half_len = tables[0].shape[0]
    lines = field.shape[3]
    both_tables = jnp.concatenate([tables[0], tables[1]], axis=1)
    halves = field.reshape(field.shape[0], field.shape[1], 2, half_len, lines)
    result = jnp.einsum("cwajl,jk->cwalk", halves, both_tables, precision=highest)
    spectra = combine_parts(result, half_len, 1.0)
    even_part = spectra[:, :, 0]
    turned = complex_mul(spectra[:, :, 1], jnp.stack([tables[2], -tables[3]]))
    joined = jnp.stack([even_part + turned, even_part - turned], axis=3)
    return joined.reshape(joined.shape[0], joined.shape[1], lines, 2 * half_len)


def inverse_columns(field, tables):
    half_len = tables[0].shape[0]
    lines = field.shape[3]
    both_tables = jnp.concatenate([tables[0], tables[1]], axis=1)
    first_half = field[:, :, :half_len]
    second_half = field[:, :, half_len:]
    twiddle = jnp.stack([tables[2][:, None], tables[3][:, None]])
    halves = jnp.stack(
        [first_half + second_half, complex_mul(first_half - second_half, twiddle)], axis=2
    )
    result = jnp.einsum("cwajl,jk->cwlak", halves, both_tables, precision=highest)
    spectra = combine_parts(result, half_len, -1.0)
    return spectra.reshape(spectra.shape[0], spectra.shape[1], lines, 2 * half_len)


def transform_forward(field, tables):
    partial_out = forward_pass(field, tables)

    def finish(piece):
        return forward_columns(piece, tables)

    return finish(lax.all_to_all(partial_out, "row", split_axis=3, concat_axis=2, tiled=True))


def transform_inverse(field, tables):
    partial_out = inverse_pass(field, tables)

    def finish(piece):
        return inverse_columns(piece, tables)

    return finish(lax.all_to_all(partial_out, "row", split_axis=3, concat_axis=2, tiled=True))


def section_forward(spectrum, multiplier, slab_obj, propagator, tables):
    wavefield = transform_inverse(complex_mul(spectrum, multiplier), tables)
    kept = []
    outgoing = wavefield
    for layer in range(slab_obj.shape[0]):
        kept.append(wavefield)
        outgoing = transform_forward(complex_mul(slab_obj[layer][:, None], wavefield), tables)
        if layer + 1 < slab_obj.shape[0]:
            wavefield = transform_inverse(complex_mul(outgoing, propagator), tables)
    return (outgoing, jnp.stack(kept))


def section_backward(adjoint, kept, multiplier, slab_obj, propagator, tables):
    layer_total = slab_obj.shape[0]
    grads = [None] * layer_total
    for layer in reversed(range(layer_total)):
        wave_adj = transform_inverse(adjoint, tables)
        grads[layer] = jnp.sum(conj_mul(wave_adj, kept[layer]), axis=1)
        field_adj = conj_mul(wave_adj, slab_obj[layer][:, None])
        backward_spec = transform_forward(field_adj, tables)
        if layer > 0:
            adjoint = conj_mul(backward_spec, propagator)
        else:
            adjoint = conj_mul(backward_spec, multiplier)
    return (adjoint, jnp.stack(grads))


def loss_adjoint(outgoing, target):
    power = outgoing[0] * outgoing[0] + outgoing[1] * outgoing[1]
    return 0.5 * (power - target)[None] * outgoing


def shards(object_slices, probe_spec, offsets, measured):
    line_count = object_slices.shape[2]
    width = object_slices.shape[3]
    half_len = width // 2
    wave_count = offsets.shape[0]
    section_count = lax.axis_size("section")
    section_pos = lax.axis_index("section")
    row_pos = lax.axis_index("row")
    index = jnp.arange(half_len, dtype=jnp.int32)
    product = index[:, None] * index[None, :] % half_len
    angle = 2.0 * math.pi / half_len * product.astype(jnp.float32)
    scale = 1.0 / math.sqrt(width)
    twid_angle = 2.0 * math.pi / width * index.astype(jnp.float32)
    tables = (
        jnp.cos(angle) * scale,
        jnp.sin(angle) * scale,
        jnp.cos(twid_angle),
        jnp.sin(twid_angle),
    )
    column_freq = row_pos * line_count + jnp.arange(line_count, dtype=jnp.int32)
    row_freq = jnp.arange(width, dtype=jnp.int32)
    column_signed = jnp.where(column_freq < half_len, column_freq, column_freq - width)
    row_signed = jnp.where(row_freq < half_len, row_freq, row_freq - width)
    square_sum = (
        column_signed[:, None] * column_signed[:, None] + row_signed[None, :] * row_signed[None, :]
    )
    phase = -math.pi * fresnel_coef / width * square_sum.astype(jnp.float32)
    propagator = jnp.stack([jnp.cos(phase), jnp.sin(phase)])[:, None]
    turns = (
        row_freq[None, None, :] * offsets[:, 0][:, None, None]
        + column_freq[None, :, None] * offsets[:, 1][:, None, None]
    ) % width
    ramp_angle = 2.0 * math.pi / width * turns.astype(jnp.float32)
    ramps = jnp.stack([jnp.cos(ramp_angle), -jnp.sin(ramp_angle)])
    start_spec = probe_spec[:, None]
    all_obj = lax.all_gather(object_slices, "section", axis=0, tiled=True)
    wave_pick = section_pos % wave_count
    ramp_pick = lax.dynamic_slice_in_dim(ramps, wave_pick, 1, axis=1)
    outgoing, kept = section_forward(start_spec, ramp_pick, all_obj, propagator, tables)
    target = lax.dynamic_slice_in_dim(measured, wave_pick, 1, axis=0)
    unused, grads = section_backward(
        loss_adjoint(outgoing, target), kept, ramp_pick, all_obj, propagator, tables
    )
    summed = lax.psum_scatter(grads, "section", scatter_dimension=0, tiled=True)
    return summed * (wave_count / section_count)


def split_table(table):
    both = np.concatenate([table.real, table.imag], axis=-1).astype(np.float32)
    high = both.astype(jnp.bfloat16)
    low = (both - high.astype(np.float32)).astype(jnp.bfloat16)
    return high, low


def fused_tables(width):
    half, quarter = width // 2, width // 4
    freq = np.arange(width)
    signed = np.where(freq < half, freq, freq - width).astype(np.float64)
    response = np.exp(-1j * np.pi * fresnel_coef / width * signed * signed)
    place = np.arange(quarter)
    place = np.where(place < quarter // 2, 2 * place, 2 * (place - quarter // 2) + 1)
    gap = place[None, :] - place[:, None]
    circ = []
    for turn in range(4):
        line = np.zeros(width, np.complex128)
        line[turn::4] = response[turn::4]
        kernel = np.fft.ifft(line)
        circ.append(kernel[gap % width])
    index = np.arange(half)
    even = np.exp(-2j * np.pi * (2 * index[:, None] * index[None, :] % width) / width)
    odd = np.exp(-2j * np.pi * ((2 * index[:, None] + 1) * index[None, :] % width) / width)
    scale = 1.0 / math.sqrt(width)
    dft = np.stack([even, odd, odd.T]) * scale
    return split_table(np.stack(circ)) + split_table(dft)


def dot_split(left, high, low):
    left_high = left.astype(jnp.bfloat16)
    left_low = (left - left_high.astype(jnp.float32)).astype(jnp.bfloat16)
    out = jnp.dot(left_low, high, preferred_element_type=jnp.float32)
    out += jnp.dot(left_high, low, preferred_element_type=jnp.float32)
    return out + jnp.dot(left_high, high, preferred_element_type=jnp.float32)


def complex_dot(left, high, low):
    out = dot_split(left, high, low)
    lines, width = out.shape[0] // 2, out.shape[1] // 2
    real = out[:lines, :width] - out[lines:, width:]
    imag = out[:lines, width:] + out[lines:, :width]
    return jnp.concatenate([real, imag], axis=0)


def times_i(value):
    lines = value.shape[0] // 2
    return jnp.concatenate([-value[lines:], value[:lines]], axis=0)


def fused_kernel(
    dims, obj_ref, spec_ref, meas_ref, ramp_y, ramp_x, circ_h, circ_l, dft_h, dft_l, out_ref,
    state, send, recv, spec_in, meas_out, meas_in, obj_out, obj_hop, obj_row, obj_col, kept,
    grad_out, grad_hop, grad_sum, grad_row, grad_col, send_sem, recv_sem, spec_sem, meas_sem,
    obj_send, hop_sem, obj_sem, pair_sem, fold_sem, grad_send, grad_sem,
):
    sections, rows, waves, layers, width = dims
    wave_rows = rows // waves
    group = sections * wave_rows
    lines = width // group
    shard = width // rows
    piece = lines // 2
    half, chunk = width // 2, width // 8
    even, odd = (layers + 1) // 2, layers // 2
    sec = lax.axis_index("section")
    row = lax.axis_index("row")
    wave = row // wave_rows
    mine = (row % wave_rows) * sections + sec
    mate = wave_rows + row - 2 * wave_rows * wave
    total = sections * rows
    me = sec * rows + row

    def place(of_wave, member):
        return member % sections, of_wave * wave_rows + member // sections

    def push(src, dst, sent, got, to_sec, to_row):
        home = jnp.logical_and(to_sec == sec, to_row == row)

        @pl.when(home)
        def _():
            pltpu.make_async_copy(src, dst, got).start()

        @pl.when(jnp.logical_not(home))
        def _():
            pltpu.make_async_remote_copy(
                src_ref=src, dst_ref=dst, send_sem=sent, recv_sem=got,
                device_id=(to_sec, to_row), device_id_type=pl.DeviceIdType.MESH,
            ).start()

    def settle(src, sent, to_sec, to_row):
        @pl.when(jnp.logical_not(jnp.logical_and(to_sec == sec, to_row == row)))
        def _():
            pltpu.make_async_copy(src, src, sent).wait()

    barrier = pltpu.get_barrier_semaphore()

    def greet(step, carry):
        other = (me + step) % total
        pl.semaphore_signal(
            barrier, inc=1, device_id=(other // rows, other % rows),
            device_id_type=pl.DeviceIdType.MESH,
        )
        return carry

    lax.fori_loop(1, total, greet, 0)
    pl.semaphore_wait(barrier, total - 1)

    own = pl.ds(pl.multiple_of(sec * piece, piece), piece)
    spec_src = spec_ref.at[:, own]
    pltpu.make_async_copy(spec_src, spec_in.at[wave], spec_sem.at[2]).start()
    push(spec_src, spec_in.at[wave], spec_sem.at[0], spec_sem.at[1], sec, mate)

    def hop_src(layer, to_sec):
        if layer % 2 == 0:
            return obj_ref.at[:, pl.ds(to_sec * piece, piece)]
        return obj_out.at[to_sec]

    def hop_dst(layer):
        if layer % 2 == 0:
            return obj_row.at[layer // 2, wave]
        return obj_hop.at[layer // 2]

    def obj_first(layer, act):
        for to_sec in range(sections):
            if act:
                push(hop_src(layer, to_sec), hop_dst(layer), obj_send.at[0], hop_sem.at[layer],
                     to_sec, row)
            else:
                settle(hop_src(layer, to_sec), obj_send.at[0], to_sec, row)

    def obj_second(layer, act):
        if layer % 2 == 0:
            src = obj_row.at[layer // 2, wave]
            if act:
                pltpu.make_async_copy(src, src, hop_sem.at[layer]).wait()
                push(src, src, obj_send.at[1 + layer], obj_sem.at[layer], sec, mate)
            else:
                settle(src, obj_send.at[1 + layer], sec, mate)
            return
        if act:
            src = obj_hop.at[layer // 2]
            pltpu.make_async_copy(src, src, hop_sem.at[layer]).wait()
        for to_row in range(rows):
            src = obj_hop.at[layer // 2, to_row % wave_rows]
            if act:
                push(src, obj_col.at[layer // 2, row], obj_send.at[1 + layer], obj_sem.at[layer],
                     sec, to_row)
            else:
                settle(src, obj_send.at[1 + layer], sec, to_row)

    def transpose_obj():
        for block in range(rows):
            for part in range(2):
                turned = obj_ref[part, :, block * shard:(block + 1) * shard].T
                for to_sec in range(sections):
                    obj_out[to_sec, block % wave_rows, block // wave_rows, :,
                            part * shard:(part + 1) * shard] = (
                        turned[to_sec * piece:(to_sec + 1) * piece]
                    )

    for layer in range(layers):
        @pl.when(sec == layer)
        def _(layer=layer):
            if layer % 2 == 1:
                transpose_obj()
            obj_first(layer, True)

    def meas_push(act):
        for to_row in range(rows):
            for side in range(2):
                src = meas_out.at[to_row // wave_rows, to_row % wave_rows + side * wave_rows, own]
                dst = meas_in.at[row, pl.ds(side * piece, piece)]
                if act:
                    push(src, dst, meas_sem.at[0], meas_sem.at[1], sec, to_row)
                else:
                    settle(src, meas_sem.at[0], sec, to_row)

    def turn_meas():
        for of_wave in range(waves):
            for block in range(rows):
                meas_out[of_wave, block] = meas_ref[of_wave, :, block * shard:(block + 1) * shard].T
        meas_push(True)

    def circ_pass():
        x = [
            jnp.concatenate(
                [state[:, b * chunk:(b + 1) * chunk],
                 state[:, half + b * chunk:half + (b + 1) * chunk]], axis=1)
            for b in range(4)
        ]
        sum_a, dif_a = x[0] + x[2], x[0] - x[2]
        sum_b, dif_b = x[1] + x[3], times_i(x[1] - x[3])
        folded = (sum_a + sum_b, dif_a - dif_b, sum_a - sum_b, dif_a + dif_b)
        y = [complex_dot(folded[t], circ_h[t], circ_l[t]) for t in range(4)]
        sum_a, dif_a = y[0] + y[2], y[0] - y[2]
        sum_b, dif_b = y[1] + y[3], times_i(y[1] - y[3])
        for b, value in enumerate((sum_a + sum_b, dif_a + dif_b, sum_a - sum_b, dif_a - dif_b)):
            state[:, b * chunk:(b + 1) * chunk] = value[:, :chunk]
            state[:, half + b * chunk:half + (b + 1) * chunk] = value[:, chunk:]

    def to_freq():
        even = complex_dot(state[:, :half], dft_h[0], dft_l[0])
        odd = complex_dot(state[:, half:], dft_h[1], dft_l[1])
        state[:, :half] = even + odd
        state[:, half:] = even - odd

    def from_freq():
        first, second = state[:, :half], state[:, half:]
        state[:, :half] = complex_dot(first + second, dft_h[0], dft_l[0])
        state[:, half:] = complex_dot(first - second, dft_h[2], dft_l[2])

    pair = 2 * lines

    def exchange(step, meanwhile=lambda: None):
        for block in range(rows):
            turned = state[:, block * pair:(block + 1) * pair].T
            side = (block // wave_rows) * piece
            for part in range(sections):
                send[step, (block % wave_rows) * sections + part, side:side + piece] = (
                    turned[part * piece:(part + 1) * piece]
                )

        def start(count, carry):
            other = (mine + count) % group
            to_sec, to_row = place(wave, other)
            pltpu.make_async_remote_copy(
                src_ref=send.at[step, other], dst_ref=recv.at[step, mine],
                send_sem=send_sem.at[step], recv_sem=recv_sem.at[step],
                device_id=(to_sec, to_row), device_id_type=pl.DeviceIdType.MESH,
            ).start()
            return carry

        lax.fori_loop(1, group, start, 0)
        recv[step, mine] = send[step, mine]
        meanwhile()
        arrived = recv.at[step, pl.ds(0, group - 1)]
        pltpu.make_async_copy(arrived, arrived, recv_sem.at[step]).wait()
        spot = lax.broadcasted_iota(jnp.int32, (lines, pair), 1) // piece
        for block in range(wave_rows):
            tiles = [recv[step, block * sections + part] for part in range(sections)]
            for which in range(4):
                out = None
                for part in range(sections):
                    turn = (part - which) % 4 * piece
                    moved = pltpu.roll(tiles[part], turn, 1) if turn else tiles[part]
                    out = moved if out is None else jnp.where(spot == part, moved, out)
                first = (which // 2) * lines
                col = (block + which % 2 * wave_rows) * pair
                state[first:first + lines, col:col + pair] = out

    def wait_object(layer):
        if layer % 2 == 0:
            buf = obj_row.at[layer // 2, 0]
        else:
            buf = obj_col.at[layer // 2]
        pltpu.make_async_copy(buf, buf, obj_sem.at[layer]).wait()

    def times_object(layer):
        for r in range(rows):
            cols = slice(r * shard, (r + 1) * shard)
            if layer % 2 == 0:
                o_re, o_im = (
                    jnp.concatenate([obj_row[layer // 2, side, part, :, cols] for side in range(2)], axis=0)
                    for part in range(2)
                )
            else:
                both = jnp.concatenate([obj_col[layer // 2, r, side] for side in range(2)], axis=0)
                o_re, o_im = both[:, :shard], both[:, shard:]
            re, im = state[:lines, cols], state[lines:, cols]
            state[:lines, cols] = o_re * re - o_im * im
            state[lines:, cols] = o_re * im + o_im * re

    def fold_src(layer):
        if layer % 2 == 0:
            return grad_out.at[layer, :, pl.ds(pl.multiple_of((1 - wave) * piece, piece), piece)]
        return grad_out.at[layer, :, :, pl.ds(pl.multiple_of((1 - wave) * half, half), half)]

    def fold_dst(layer):
        if layer % 2 == 0:
            return grad_hop.at[layer // 2]
        return grad_sum.at[layer // 2]

    def grad_first(layer):
        push(fold_src(layer), fold_dst(layer), pair_sem.at[layer], fold_sem.at[layer], sec, mate)

    def last_push(layer, act):
        if layer % 2 == 0:
            src = grad_hop.at[even + layer // 2]
            if act:
                push(src, grad_row.at[sec], grad_send.at[layer], grad_sem.at[0], layer, row)
            else:
                settle(src, grad_send.at[layer], layer, row)
            return
        for part in range(wave_rows):
            to_row = wave * wave_rows + part
            src = grad_sum.at[odd + layer // 2, :, :, pl.ds(part * shard, shard)]
            dst = grad_col.at[row % wave_rows, sec]
            if act:
                push(src, dst, grad_send.at[layer], grad_sem.at[0], layer, to_row)
            else:
                settle(src, grad_send.at[layer], layer, to_row)

    def grad_second(layer):
        came = fold_dst(layer)
        pltpu.make_async_copy(came, came, fold_sem.at[layer]).wait()
        if layer % 2 == 0:
            held = grad_out[layer, :, pl.ds(pl.multiple_of(wave * piece, piece), piece)]
            grad_hop[even + layer // 2] = grad_hop[layer // 2] + held
        else:
            held = grad_out[layer, :, :, pl.ds(pl.multiple_of(wave * half, half), half)]
            grad_sum[odd + layer // 2] = grad_sum[layer // 2] + held
        last_push(layer, True)

    def gradient(layer):
        for r in range(rows):
            cols = slice(r * shard, (r + 1) * shard)
            re, im = state[:lines, cols], state[lines:, cols]
            k_re, k_im = kept[layer, :lines, cols], kept[layer, lines:, cols]
            grad_out[layer, 0, :, cols] = re * k_re - im * k_im
            grad_out[layer, 1, :, cols] = -(re * k_im + im * k_re)

    pltpu.make_async_copy(spec_in.at[0], spec_in.at[0], spec_sem.at[1]).wait()
    pltpu.make_async_copy(spec_in.at[0], spec_in.at[0], spec_sem.at[2]).wait()
    y_re, y_im = ramp_y[0], ramp_y[1]
    x_re, x_im = ramp_x[0], ramp_x[1]
    turn_re = x_re * y_re - x_im * y_im
    turn_im = x_re * y_im + x_im * y_re
    p_re, p_im = (
        jnp.concatenate([spec_in[side, part] for side in range(2)], axis=0) for part in range(2)
    )
    state[:lines] = p_re * turn_re + p_im * turn_im
    state[lines:] = p_re * turn_im - p_im * turn_re
    from_freq()

    def first_objects():
        obj_second(0, True)
        turn_meas()
        obj_second(1, True)

    exchange(0, first_objects)
    from_freq()
    state[lines:] = -state[lines:]
    for layer in range(layers):
        kept[layer] = state[...]
        wait_object(layer)
        times_object(layer)
        if layer + 1 < layers:
            circ_pass()
            later = layer + 2
            if later < layers:
                exchange(1 + layer, lambda later=later: obj_second(later, True))
            else:
                exchange(1 + layer)
            circ_pass()
    to_freq()
    exchange(layers)
    to_freq()
    pltpu.make_async_copy(meas_in, meas_in, meas_sem.at[1]).wait()
    for r in range(rows):
        cols = slice(r * shard, (r + 1) * shard)
        re, im = state[:lines, cols], state[lines:, cols]
        weight = 0.5 * (re * re + im * im - meas_in[r])
        state[:lines, cols] = weight * re
        state[lines:, cols] = -(weight * im)
    from_freq()
    exchange(layers + 1)
    from_freq()
    for layer in reversed(range(layers)):
        gradient(layer)
        if layer > 0:
            times_object(layer)
            circ_pass()

            def gradients(layer=layer):
                grad_first(layer)
                if layer + 1 < layers:
                    grad_second(layer + 1)

            exchange(layers + 1 + layers - layer, gradients)
            circ_pass()

    grad_first(0)
    grad_second(1)
    grad_second(0)

    settle(spec_src, spec_sem.at[0], sec, mate)
    meas_push(False)
    for layer in range(layers):
        settle(fold_src(layer), pair_sem.at[layer], sec, mate)
        last_push(layer, False)
        obj_second(layer, False)

        @pl.when(sec == layer)
        def _(layer=layer):
            obj_first(layer, False)
    for step in range(2 * layers + 1):
        gone = send.at[step, pl.ds(0, group - 1)]
        pltpu.make_async_copy(gone, gone, send_sem.at[step]).wait()

    @pl.when(sec % 2 == 0)
    def _():
        pltpu.make_async_copy(grad_row, grad_row, grad_sem.at[0]).wait()
        for part in range(sections):
            out_ref[:, part * piece:(part + 1) * piece] = grad_row[part]

    @pl.when(sec % 2 == 1)
    def _():
        pltpu.make_async_copy(grad_col, grad_col, grad_sem.at[0]).wait()
        for block in range(rows):
            side = (block // wave_rows) * piece
            for part in range(2):
                joined = jnp.concatenate(
                    [grad_col[block % wave_rows, member, part, side:side + piece]
                     for member in range(sections)], axis=0)
                out_ref[part, :, block * pair:(block + 1) * pair] = joined.T


def fused_shards(object_slices, probe_spec, offsets, measured):
    sections, rows = lax.axis_size("section"), lax.axis_size("row")
    width = object_slices.shape[3]
    waves = offsets.shape[0]
    layers = sections * object_slices.shape[0]
    dims = (sections, rows, waves, layers, width)
    wave_rows = rows // waves
    group = sections * wave_rows
    lines = width // group
    shard = width // rows
    row = lax.axis_index("row")
    shift = lax.dynamic_index_in_dim(offsets, row // wave_rows, 0, keepdims=False)
    unit = 2.0 * math.pi / width
    turn_y = unit * (jnp.arange(width, dtype=jnp.int32) * shift[0] % width).astype(jnp.float32)
    piece = lines // 2
    inner = jnp.arange(lines, dtype=jnp.int32)
    line = (row % wave_rows + wave_rows * (inner // piece)) * shard
    line = line + lax.axis_index("section") * piece + inner % piece
    turn_x = unit * (line * shift[1] % width).astype(jnp.float32)
    ramp_y = jnp.stack([jnp.cos(turn_y), jnp.sin(turn_y)])[:, None, :]
    ramp_x = jnp.stack([jnp.cos(turn_x), jnp.sin(turn_x)])[:, :, None]
    tables = [jnp.asarray(t) for t in fused_tables(width)]
    steps = 2 * layers + 1
    f32 = jnp.float32
    vmem = pl.BlockSpec(memory_space=pltpu.VMEM)
    even, odd = (layers + 1) // 2, layers // 2
    dma = pltpu.SemaphoreType.DMA
    result = pl.pallas_call(
        lambda *refs: fused_kernel(dims, *refs),
        out_shape=jax.ShapeDtypeStruct((2, shard, width), f32),
        in_specs=[vmem] * 9,
        out_specs=vmem,
        scratch_shapes=[
            pltpu.VMEM((2 * lines, width), f32),
            pltpu.VMEM((steps, group, lines, 2 * lines), f32),
            pltpu.VMEM((steps, group, lines, 2 * lines), f32),
            pltpu.VMEM((2, 2, piece, width), f32),
            pltpu.VMEM((waves, rows, shard, shard), f32),
            pltpu.VMEM((rows, lines, shard), f32),
            pltpu.VMEM((sections, wave_rows, 2, piece, 2 * shard), f32),
            pltpu.VMEM((odd, wave_rows, 2, piece, 2 * shard), f32),
            pltpu.VMEM((even, 2, 2, piece, width), f32),
            pltpu.VMEM((odd, rows, 2, piece, 2 * shard), f32),
            pltpu.VMEM((layers, 2 * lines, width), f32),
            pltpu.VMEM((layers, 2, lines, width), f32),
            pltpu.VMEM((2 * even, 2, piece, width), f32),
            pltpu.VMEM((2 * odd, 2, lines, width // 2), f32),
            pltpu.VMEM((sections, 2, piece, width), f32),
            pltpu.VMEM((wave_rows, sections, 2, lines, shard), f32),
            dma((steps,)),
            dma((steps,)),
            dma((3,)),
            dma((2,)),
            dma((1 + layers,)),
            dma((layers,)),
            dma((layers,)),
            dma((layers,)),
            dma((layers,)),
            dma((layers,)),
            dma((1,)),
        ],
        compiler_params=pltpu.CompilerParams(
            collective_id=0, has_side_effects=True, vmem_limit_bytes=60 * 1024 * 1024
        ),
    )(object_slices[0], probe_spec, measured, ramp_y, ramp_x, *tables)
    return result[None]


def fused_fits(sections, rows, waves, layers, width):
    if rows % waves or layers != sections or layers % 2:
        return False
    group = sections * rows // waves
    if width % group or width % rows or group % sections:
        return False
    lines, shard = width // group, width // rows
    if 2 * lines != 128 or shard != 2 * lines or width % 1024:
        return False
    return waves == 2 and sections == 4


def solution(mesh):
    placed = (P("section", None, "row", None), P(None, "row", None), P(), P(None, "row", None))

    def build(body):
        return jax.shard_map(
            body,
            mesh=mesh,
            in_specs=placed,
            out_specs=P("section", None, "row", None),
            check_vma=False,
        )

    def run(object_slices, probe_spec, offsets, measured):
        fits = fused_fits(
            mesh.shape["section"], mesh.shape["row"], offsets.shape[0],
            object_slices.shape[0], object_slices.shape[3],
        )
        body = fused_shards if fits else shards
        return build(body)(object_slices, probe_spec, offsets, measured)

    return run
```

```python
import math

import jax
import jax.numpy as jnp
import numpy as np
from jax import lax
from jax.experimental import pallas as pl
from jax.experimental.pallas import tpu as pltpu
from jax.sharding import PartitionSpec as P

fresnel_coef = 0.37
highest = lax.Precision.HIGHEST


def complex_mul(left, right):
    return jnp.stack(
        [left[0] * right[0] - left[1] * right[1], left[0] * right[1] + left[1] * right[0]]
    )


def conj_mul(left, right):
    return jnp.stack(
        [left[0] * right[0] + left[1] * right[1], left[1] * right[0] - left[0] * right[1]]
    )


def combine_parts(result, half_len, direction):
    first = result[..., :half_len]
    second = result[..., half_len:]
    return jnp.stack([first[0] + direction * second[1], first[1] - direction * second[0]])


def small_dft(stacked, tables, direction):
    half_len = tables[0].shape[0]
    both_tables = jnp.concatenate([tables[0], tables[1]], axis=1)
    flat = stacked.reshape(-1, half_len)
    result = jnp.dot(flat, both_tables, precision=highest)
    result = result.reshape(stacked.shape[:-1] + (2 * half_len,))
    return combine_parts(result, half_len, direction)


def forward_pass(field, tables):
    half_len = tables[0].shape[0]
    halves = field.reshape(field.shape[0], field.shape[1], field.shape[2], 2, half_len)
    spectra = small_dft(halves, tables, 1.0)
    even_part = spectra[:, :, :, 0]
    turned = complex_mul(spectra[:, :, :, 1], jnp.stack([tables[2], -tables[3]]))
    joined = jnp.stack([even_part + turned, even_part - turned], axis=3)
    return joined.reshape(joined.shape[0], joined.shape[1], joined.shape[2], 2 * half_len)


def inverse_pass(field, tables):
    half_len = tables[0].shape[0]
    first_half = field[:, :, :, :half_len]
    second_half = field[:, :, :, half_len:]
    twiddle = jnp.stack([tables[2], tables[3]])
    halves = jnp.stack(
        [first_half + second_half, complex_mul(first_half - second_half, twiddle)], axis=3
    )
    spectra = small_dft(halves, tables, -1.0)
    return spectra.reshape(spectra.shape[0], spectra.shape[1], spectra.shape[2], 2 * half_len)


def forward_columns(field, tables):
    half_len = tables[0].shape[0]
    lines = field.shape[3]
    both_tables = jnp.concatenate([tables[0], tables[1]], axis=1)
    halves = field.reshape(field.shape[0], field.shape[1], 2, half_len, lines)
    result = jnp.einsum("cwajl,jk->cwalk", halves, both_tables, precision=highest)
    spectra = combine_parts(result, half_len, 1.0)
    even_part = spectra[:, :, 0]
    turned = complex_mul(spectra[:, :, 1], jnp.stack([tables[2], -tables[3]]))
    joined = jnp.stack([even_part + turned, even_part - turned], axis=3)
    return joined.reshape(joined.shape[0], joined.shape[1], lines, 2 * half_len)


def inverse_columns(field, tables):
    half_len = tables[0].shape[0]
    lines = field.shape[3]
    both_tables = jnp.concatenate([tables[0], tables[1]], axis=1)
    first_half = field[:, :, :half_len]
    second_half = field[:, :, half_len:]
    twiddle = jnp.stack([tables[2][:, None], tables[3][:, None]])
    halves = jnp.stack(
        [first_half + second_half, complex_mul(first_half - second_half, twiddle)], axis=2
    )
    result = jnp.einsum("cwajl,jk->cwlak", halves, both_tables, precision=highest)
    spectra = combine_parts(result, half_len, -1.0)
    return spectra.reshape(spectra.shape[0], spectra.shape[1], lines, 2 * half_len)


def transform_forward(field, tables):
    partial_out = forward_pass(field, tables)

    def finish(piece):
        return forward_columns(piece, tables)

    return finish(lax.all_to_all(partial_out, "row", split_axis=3, concat_axis=2, tiled=True))


def transform_inverse(field, tables):
    partial_out = inverse_pass(field, tables)

    def finish(piece):
        return inverse_columns(piece, tables)

    return finish(lax.all_to_all(partial_out, "row", split_axis=3, concat_axis=2, tiled=True))


def section_forward(spectrum, multiplier, slab_obj, propagator, tables):
    wavefield = transform_inverse(complex_mul(spectrum, multiplier), tables)
    kept = []
    outgoing = wavefield
    for layer in range(slab_obj.shape[0]):
        kept.append(wavefield)
        outgoing = transform_forward(complex_mul(slab_obj[layer][:, None], wavefield), tables)
        if layer + 1 < slab_obj.shape[0]:
            wavefield = transform_inverse(complex_mul(outgoing, propagator), tables)
    return (outgoing, jnp.stack(kept))


def section_backward(adjoint, kept, multiplier, slab_obj, propagator, tables):
    layer_total = slab_obj.shape[0]
    grads = [None] * layer_total
    for layer in reversed(range(layer_total)):
        wave_adj = transform_inverse(adjoint, tables)
        grads[layer] = jnp.sum(conj_mul(wave_adj, kept[layer]), axis=1)
        field_adj = conj_mul(wave_adj, slab_obj[layer][:, None])
        backward_spec = transform_forward(field_adj, tables)
        if layer > 0:
            adjoint = conj_mul(backward_spec, propagator)
        else:
            adjoint = conj_mul(backward_spec, multiplier)
    return (adjoint, jnp.stack(grads))


def loss_adjoint(outgoing, target):
    power = outgoing[0] * outgoing[0] + outgoing[1] * outgoing[1]
    return 0.5 * (power - target)[None] * outgoing


def shards(object_slices, probe_spec, offsets, measured):
    line_count = object_slices.shape[2]
    width = object_slices.shape[3]
    half_len = width // 2
    wave_count = offsets.shape[0]
    section_count = lax.axis_size("section")
    section_pos = lax.axis_index("section")
    row_pos = lax.axis_index("row")
    index = jnp.arange(half_len, dtype=jnp.int32)
    product = index[:, None] * index[None, :] % half_len
    angle = 2.0 * math.pi / half_len * product.astype(jnp.float32)
    scale = 1.0 / math.sqrt(width)
    twid_angle = 2.0 * math.pi / width * index.astype(jnp.float32)
    tables = (
        jnp.cos(angle) * scale,
        jnp.sin(angle) * scale,
        jnp.cos(twid_angle),
        jnp.sin(twid_angle),
    )
    column_freq = row_pos * line_count + jnp.arange(line_count, dtype=jnp.int32)
    row_freq = jnp.arange(width, dtype=jnp.int32)
    column_signed = jnp.where(column_freq < half_len, column_freq, column_freq - width)
    row_signed = jnp.where(row_freq < half_len, row_freq, row_freq - width)
    square_sum = (
        column_signed[:, None] * column_signed[:, None] + row_signed[None, :] * row_signed[None, :]
    )
    phase = -math.pi * fresnel_coef / width * square_sum.astype(jnp.float32)
    propagator = jnp.stack([jnp.cos(phase), jnp.sin(phase)])[:, None]
    turns = (
        row_freq[None, None, :] * offsets[:, 0][:, None, None]
        + column_freq[None, :, None] * offsets[:, 1][:, None, None]
    ) % width
    ramp_angle = 2.0 * math.pi / width * turns.astype(jnp.float32)
    ramps = jnp.stack([jnp.cos(ramp_angle), -jnp.sin(ramp_angle)])
    start_spec = probe_spec[:, None]
    all_obj = lax.all_gather(object_slices, "section", axis=0, tiled=True)
    wave_pick = section_pos % wave_count
    ramp_pick = lax.dynamic_slice_in_dim(ramps, wave_pick, 1, axis=1)
    outgoing, kept = section_forward(start_spec, ramp_pick, all_obj, propagator, tables)
    target = lax.dynamic_slice_in_dim(measured, wave_pick, 1, axis=0)
    unused, grads = section_backward(
        loss_adjoint(outgoing, target), kept, ramp_pick, all_obj, propagator, tables
    )
    summed = lax.psum_scatter(grads, "section", scatter_dimension=0, tiled=True)
    return summed * (wave_count / section_count)


def split_table(table):
    both = np.concatenate([table.real, table.imag], axis=-1).astype(np.float32)
    high = both.astype(jnp.bfloat16)
    low = (both - high.astype(np.float32)).astype(jnp.bfloat16)
    return high, low


def fused_tables(width):
    half, quarter = width // 2, width // 4
    freq = np.arange(width)
    signed = np.where(freq < half, freq, freq - width).astype(np.float64)
    response = np.exp(-1j * np.pi * fresnel_coef / width * signed * signed)
    place = np.arange(quarter)
    place = np.where(place < quarter // 2, 2 * place, 2 * (place - quarter // 2) + 1)
    gap = place[None, :] - place[:, None]
    circ = []
    for turn in range(4):
        line = np.zeros(width, np.complex128)
        line[turn::4] = response[turn::4]
        kernel = np.fft.ifft(line)
        circ.append(kernel[gap % width])
    index = np.arange(half)
    even = np.exp(-2j * np.pi * (2 * index[:, None] * index[None, :] % width) / width)
    odd = np.exp(-2j * np.pi * ((2 * index[:, None] + 1) * index[None, :] % width) / width)
    scale = 1.0 / math.sqrt(width)
    dft = np.stack([even, odd, odd.T]) * scale
    return split_table(np.stack(circ)) + split_table(dft)


def dot_split(left, high, low):
    left_high = left.astype(jnp.bfloat16)
    left_low = (left - left_high.astype(jnp.float32)).astype(jnp.bfloat16)
    out = jnp.dot(left_low, high, preferred_element_type=jnp.float32)
    out += jnp.dot(left_high, low, preferred_element_type=jnp.float32)
    return out + jnp.dot(left_high, high, preferred_element_type=jnp.float32)


def complex_dot(left, high, low):
    out = dot_split(left, high, low)
    lines, width = out.shape[0] // 2, out.shape[1] // 2
    real = out[:lines, :width] - out[lines:, width:]
    imag = out[:lines, width:] + out[lines:, :width]
    return jnp.concatenate([real, imag], axis=0)


def times_i(value):
    lines = value.shape[0] // 2
    return jnp.concatenate([-value[lines:], value[:lines]], axis=0)


def fused_kernel(
    dims, obj_ref, spec_ref, meas_ref, ramp_y, ramp_x, circ_h, circ_l, dft_h, dft_l, out_ref,
    state, send, recv, spec_in, meas_out, meas_in, obj_out, obj_hop, obj_row, obj_col, kept,
    grad_out, grad_hop, grad_sum, grad_row, grad_col, send_sem, recv_sem, spec_sem, meas_sem,
    obj_send, hop_sem, obj_sem, pair_sem, fold_sem, grad_send, grad_sem,
):
    sections, rows, waves, layers, width = dims
    wave_rows = rows // waves
    group = sections * wave_rows
    lines = width // group
    shard = width // rows
    piece = lines // 2
    half, chunk = width // 2, width // 8
    even, odd = (layers + 1) // 2, layers // 2
    sec = lax.axis_index("section")
    row = lax.axis_index("row")
    wave = row // wave_rows
    mine = (row % wave_rows) * sections + sec
    mate = wave_rows + row - 2 * wave_rows * wave
    total = sections * rows
    me = sec * rows + row

    def place(of_wave, member):
        return member % sections, of_wave * wave_rows + member // sections

    def push(src, dst, sent, got, to_sec, to_row):
        home = jnp.logical_and(to_sec == sec, to_row == row)

        @pl.when(home)
        def _():
            pltpu.make_async_copy(src, dst, got).start()

        @pl.when(jnp.logical_not(home))
        def _():
            pltpu.make_async_remote_copy(
                src_ref=src, dst_ref=dst, send_sem=sent, recv_sem=got,
                device_id=(to_sec, to_row), device_id_type=pl.DeviceIdType.MESH,
            ).start()

    def settle(src, sent, to_sec, to_row):
        @pl.when(jnp.logical_not(jnp.logical_and(to_sec == sec, to_row == row)))
        def _():
            pltpu.make_async_copy(src, src, sent).wait()

    barrier = pltpu.get_barrier_semaphore()

    def greet(step, carry):
        other = (me + step) % total
        pl.semaphore_signal(
            barrier, inc=1, device_id=(other // rows, other % rows),
            device_id_type=pl.DeviceIdType.MESH,
        )
        return carry

    lax.fori_loop(1, total, greet, 0)
    pl.semaphore_wait(barrier, total - 1)

    own = pl.ds(pl.multiple_of(sec * piece, piece), piece)
    spec_src = spec_ref.at[:, own]
    pltpu.make_async_copy(spec_src, spec_in.at[wave], spec_sem.at[2]).start()
    push(spec_src, spec_in.at[wave], spec_sem.at[0], spec_sem.at[1], sec, mate)

    def hop_src(layer, to_sec):
        if layer % 2 == 0:
            return obj_ref.at[:, pl.ds(to_sec * piece, piece)]
        return obj_out.at[to_sec]

    def hop_dst(layer):
        if layer % 2 == 0:
            return obj_row.at[layer // 2, wave]
        return obj_hop.at[layer // 2]

    def obj_first(layer, act):
        for to_sec in range(sections):
            if act:
                push(hop_src(layer, to_sec), hop_dst(layer), obj_send.at[0], hop_sem.at[layer],
                     to_sec, row)
            else:
                settle(hop_src(layer, to_sec), obj_send.at[0], to_sec, row)

    def obj_second(layer, act):
        if layer % 2 == 0:
            src = obj_row.at[layer // 2, wave]
            if act:
                pltpu.make_async_copy(src, src, hop_sem.at[layer]).wait()
                push(src, src, obj_send.at[1 + layer], obj_sem.at[layer], sec, mate)
            else:
                settle(src, obj_send.at[1 + layer], sec, mate)
            return
        if act:
            src = obj_hop.at[layer // 2]
            pltpu.make_async_copy(src, src, hop_sem.at[layer]).wait()
        for to_row in range(rows):
            src = obj_hop.at[layer // 2, to_row % wave_rows]
            if act:
                push(src, obj_col.at[layer // 2, row], obj_send.at[1 + layer], obj_sem.at[layer],
                     sec, to_row)
            else:
                settle(src, obj_send.at[1 + layer], sec, to_row)

    def transpose_obj():
        for block in range(rows):
            for part in range(2):
                turned = obj_ref[part, :, block * shard:(block + 1) * shard].T
                for to_sec in range(sections):
                    obj_out[to_sec, block % wave_rows, block // wave_rows, :,
                            part * shard:(part + 1) * shard] = (
                        turned[to_sec * piece:(to_sec + 1) * piece]
                    )

    for layer in range(layers):
        @pl.when(sec == layer)
        def _(layer=layer):
            if layer % 2 == 1:
                transpose_obj()
            obj_first(layer, True)

    def meas_push(act):
        for to_row in range(rows):
            for side in range(2):
                src = meas_out.at[to_row // wave_rows, to_row % wave_rows + side * wave_rows, own]
                dst = meas_in.at[row, pl.ds(side * piece, piece)]
                if act:
                    push(src, dst, meas_sem.at[0], meas_sem.at[1], sec, to_row)
                else:
                    settle(src, meas_sem.at[0], sec, to_row)

    def turn_meas():
        for of_wave in range(waves):
            for block in range(rows):
                meas_out[of_wave, block] = meas_ref[of_wave, :, block * shard:(block + 1) * shard].T
        meas_push(True)

    def circ_pass():
        x = [
            jnp.concatenate(
                [state[:, b * chunk:(b + 1) * chunk],
                 state[:, half + b * chunk:half + (b + 1) * chunk]], axis=1)
            for b in range(4)
        ]
        sum_a, dif_a = x[0] + x[2], x[0] - x[2]
        sum_b, dif_b = x[1] + x[3], times_i(x[1] - x[3])
        folded = (sum_a + sum_b, dif_a - dif_b, sum_a - sum_b, dif_a + dif_b)
        y = [complex_dot(folded[t], circ_h[t], circ_l[t]) for t in range(4)]
        sum_a, dif_a = y[0] + y[2], y[0] - y[2]
        sum_b, dif_b = y[1] + y[3], times_i(y[1] - y[3])
        for b, value in enumerate((sum_a + sum_b, dif_a + dif_b, sum_a - sum_b, dif_a - dif_b)):
            state[:, b * chunk:(b + 1) * chunk] = value[:, :chunk]
            state[:, half + b * chunk:half + (b + 1) * chunk] = value[:, chunk:]

    def to_freq():
        even = complex_dot(state[:, :half], dft_h[0], dft_l[0])
        odd = complex_dot(state[:, half:], dft_h[1], dft_l[1])
        state[:, :half] = even + odd
        state[:, half:] = even - odd

    def from_freq():
        first, second = state[:, :half], state[:, half:]
        state[:, :half] = complex_dot(first + second, dft_h[0], dft_l[0])
        state[:, half:] = complex_dot(first - second, dft_h[2], dft_l[2])

    pair = 2 * lines

    def exchange(step, meanwhile=lambda: None):
        for block in range(rows):
            turned = state[:, block * pair:(block + 1) * pair].T
            side = (block // wave_rows) * piece
            for part in range(sections):
                send[step, (block % wave_rows) * sections + part, side:side + piece] = (
                    turned[part * piece:(part + 1) * piece]
                )

        def start(count, carry):
            code = group - count
            spot = row % wave_rows
            to_sec = (sec // 2 + code // 4) % 2 * 2 + (sec + code // 2) % 2
            to_spot = (spot // 2 + code // 8) % 2 * 2 + (spot + code) % 2
            to_row = wave * wave_rows + to_spot
            other = to_spot * sections + to_sec
            pltpu.make_async_remote_copy(
                src_ref=send.at[step, other], dst_ref=recv.at[step, mine],
                send_sem=send_sem.at[step], recv_sem=recv_sem.at[step],
                device_id=(to_sec, to_row), device_id_type=pl.DeviceIdType.MESH,
            ).start()
            return carry

        lax.fori_loop(1, group, start, 0)
        recv[step, mine] = send[step, mine]
        meanwhile()
        arrived = recv.at[step, pl.ds(0, group - 1)]
        pltpu.make_async_copy(arrived, arrived, recv_sem.at[step]).wait()
        spot = lax.broadcasted_iota(jnp.int32, (lines, pair), 1) // piece
        for block in range(wave_rows):
            tiles = [recv[step, block * sections + part] for part in range(sections)]
            for which in range(4):
                out = None
                for part in range(sections):
                    turn = (part - which) % 4 * piece
                    moved = pltpu.roll(tiles[part], turn, 1) if turn else tiles[part]
                    out = moved if out is None else jnp.where(spot == part, moved, out)
                first = (which // 2) * lines
                col = (block + which % 2 * wave_rows) * pair
                state[first:first + lines, col:col + pair] = out

    def wait_object(layer):
        if layer % 2 == 0:
            buf = obj_row.at[layer // 2, 0]
        else:
            buf = obj_col.at[layer // 2]
        pltpu.make_async_copy(buf, buf, obj_sem.at[layer]).wait()

    def times_object(layer):
        for r in range(rows):
            cols = slice(r * shard, (r + 1) * shard)
            if layer % 2 == 0:
                o_re, o_im = (
                    jnp.concatenate([obj_row[layer // 2, side, part, :, cols] for side in range(2)], axis=0)
                    for part in range(2)
                )
            else:
                both = jnp.concatenate([obj_col[layer // 2, r, side] for side in range(2)], axis=0)
                o_re, o_im = both[:, :shard], both[:, shard:]
            re, im = state[:lines, cols], state[lines:, cols]
            state[:lines, cols] = o_re * re - o_im * im
            state[lines:, cols] = o_re * im + o_im * re

    def fold_src(layer):
        if layer % 2 == 0:
            return grad_out.at[layer, :, pl.ds(pl.multiple_of((1 - wave) * piece, piece), piece)]
        return grad_out.at[layer, :, :, pl.ds(pl.multiple_of((1 - wave) * half, half), half)]

    def fold_dst(layer):
        if layer % 2 == 0:
            return grad_hop.at[layer // 2]
        return grad_sum.at[layer // 2]

    def grad_first(layer):
        push(fold_src(layer), fold_dst(layer), pair_sem.at[layer], fold_sem.at[layer], sec, mate)

    def last_push(layer, act):
        if layer % 2 == 0:
            src = grad_hop.at[even + layer // 2]
            if act:
                push(src, grad_row.at[sec], grad_send.at[layer], grad_sem.at[0], layer, row)
            else:
                settle(src, grad_send.at[layer], layer, row)
            return
        for part in range(wave_rows):
            to_row = wave * wave_rows + part
            src = grad_sum.at[odd + layer // 2, :, :, pl.ds(part * shard, shard)]
            dst = grad_col.at[row % wave_rows, sec]
            if act:
                push(src, dst, grad_send.at[layer], grad_sem.at[0], layer, to_row)
            else:
                settle(src, grad_send.at[layer], layer, to_row)

    def grad_second(layer):
        came = fold_dst(layer)
        pltpu.make_async_copy(came, came, fold_sem.at[layer]).wait()
        if layer % 2 == 0:
            held = grad_out[layer, :, pl.ds(pl.multiple_of(wave * piece, piece), piece)]
            grad_hop[even + layer // 2] = grad_hop[layer // 2] + held
        else:
            held = grad_out[layer, :, :, pl.ds(pl.multiple_of(wave * half, half), half)]
            grad_sum[odd + layer // 2] = grad_sum[layer // 2] + held
        last_push(layer, True)

    def gradient(layer):
        for r in range(rows):
            cols = slice(r * shard, (r + 1) * shard)
            re, im = state[:lines, cols], state[lines:, cols]
            k_re, k_im = kept[layer, :lines, cols], kept[layer, lines:, cols]
            grad_out[layer, 0, :, cols] = re * k_re - im * k_im
            grad_out[layer, 1, :, cols] = -(re * k_im + im * k_re)

    pltpu.make_async_copy(spec_in.at[0], spec_in.at[0], spec_sem.at[1]).wait()
    pltpu.make_async_copy(spec_in.at[0], spec_in.at[0], spec_sem.at[2]).wait()
    y_re, y_im = ramp_y[0], ramp_y[1]
    x_re, x_im = ramp_x[0], ramp_x[1]
    turn_re = x_re * y_re - x_im * y_im
    turn_im = x_re * y_im + x_im * y_re
    p_re, p_im = (
        jnp.concatenate([spec_in[side, part] for side in range(2)], axis=0) for part in range(2)
    )
    state[:lines] = p_re * turn_re + p_im * turn_im
    state[lines:] = p_re * turn_im - p_im * turn_re
    from_freq()

    def first_objects():
        obj_second(0, True)
        turn_meas()
        obj_second(1, True)

    exchange(0, first_objects)
    from_freq()
    state[lines:] = -state[lines:]
    for layer in range(layers):
        kept[layer] = state[...]
        wait_object(layer)
        times_object(layer)
        if layer + 1 < layers:
            circ_pass()
            later = layer + 2
            if later < layers:
                exchange(1 + layer, lambda later=later: obj_second(later, True))
            else:
                exchange(1 + layer)
            circ_pass()
    to_freq()
    exchange(layers)
    to_freq()
    pltpu.make_async_copy(meas_in, meas_in, meas_sem.at[1]).wait()
    for r in range(rows):
        cols = slice(r * shard, (r + 1) * shard)
        re, im = state[:lines, cols], state[lines:, cols]
        weight = 0.5 * (re * re + im * im - meas_in[r])
        state[:lines, cols] = weight * re
        state[lines:, cols] = -(weight * im)
    from_freq()
    exchange(layers + 1)
    from_freq()
    for layer in reversed(range(layers)):
        gradient(layer)
        if layer > 0:
            times_object(layer)
            circ_pass()

            def gradients(layer=layer):
                grad_first(layer)
                if layer + 1 < layers:
                    grad_second(layer + 1)

            exchange(layers + 1 + layers - layer, gradients)
            circ_pass()

    grad_first(0)
    grad_second(1)
    grad_second(0)

    settle(spec_src, spec_sem.at[0], sec, mate)
    meas_push(False)
    for layer in range(layers):
        settle(fold_src(layer), pair_sem.at[layer], sec, mate)
        last_push(layer, False)
        obj_second(layer, False)

        @pl.when(sec == layer)
        def _(layer=layer):
            obj_first(layer, False)
    for step in range(2 * layers + 1):
        gone = send.at[step, pl.ds(0, group - 1)]
        pltpu.make_async_copy(gone, gone, send_sem.at[step]).wait()

    @pl.when(sec % 2 == 0)
    def _():
        pltpu.make_async_copy(grad_row, grad_row, grad_sem.at[0]).wait()
        for part in range(sections):
            out_ref[:, part * piece:(part + 1) * piece] = grad_row[part]

    @pl.when(sec % 2 == 1)
    def _():
        pltpu.make_async_copy(grad_col, grad_col, grad_sem.at[0]).wait()
        for block in range(rows):
            side = (block // wave_rows) * piece
            for part in range(2):
                joined = jnp.concatenate(
                    [grad_col[block % wave_rows, member, part, side:side + piece]
                     for member in range(sections)], axis=0)
                out_ref[part, :, block * pair:(block + 1) * pair] = joined.T


def fused_shards(object_slices, probe_spec, offsets, measured):
    sections, rows = lax.axis_size("section"), lax.axis_size("row")
    width = object_slices.shape[3]
    waves = offsets.shape[0]
    layers = sections * object_slices.shape[0]
    dims = (sections, rows, waves, layers, width)
    wave_rows = rows // waves
    group = sections * wave_rows
    lines = width // group
    shard = width // rows
    row = lax.axis_index("row")
    shift = lax.dynamic_index_in_dim(offsets, row // wave_rows, 0, keepdims=False)
    unit = 2.0 * math.pi / width
    turn_y = unit * (jnp.arange(width, dtype=jnp.int32) * shift[0] % width).astype(jnp.float32)
    piece = lines // 2
    inner = jnp.arange(lines, dtype=jnp.int32)
    line = (row % wave_rows + wave_rows * (inner // piece)) * shard
    line = line + lax.axis_index("section") * piece + inner % piece
    turn_x = unit * (line * shift[1] % width).astype(jnp.float32)
    ramp_y = jnp.stack([jnp.cos(turn_y), jnp.sin(turn_y)])[:, None, :]
    ramp_x = jnp.stack([jnp.cos(turn_x), jnp.sin(turn_x)])[:, :, None]
    tables = [jnp.asarray(t) for t in fused_tables(width)]
    steps = 2 * layers + 1
    f32 = jnp.float32
    vmem = pl.BlockSpec(memory_space=pltpu.VMEM)
    even, odd = (layers + 1) // 2, layers // 2
    dma = pltpu.SemaphoreType.DMA
    result = pl.pallas_call(
        lambda *refs: fused_kernel(dims, *refs),
        out_shape=jax.ShapeDtypeStruct((2, shard, width), f32),
        in_specs=[vmem] * 9,
        out_specs=vmem,
        scratch_shapes=[
            pltpu.VMEM((2 * lines, width), f32),
            pltpu.VMEM((steps, group, lines, 2 * lines), f32),
            pltpu.VMEM((steps, group, lines, 2 * lines), f32),
            pltpu.VMEM((2, 2, piece, width), f32),
            pltpu.VMEM((waves, rows, shard, shard), f32),
            pltpu.VMEM((rows, lines, shard), f32),
            pltpu.VMEM((sections, wave_rows, 2, piece, 2 * shard), f32),
            pltpu.VMEM((odd, wave_rows, 2, piece, 2 * shard), f32),
            pltpu.VMEM((even, 2, 2, piece, width), f32),
            pltpu.VMEM((odd, rows, 2, piece, 2 * shard), f32),
            pltpu.VMEM((layers, 2 * lines, width), f32),
            pltpu.VMEM((layers, 2, lines, width), f32),
            pltpu.VMEM((2 * even, 2, piece, width), f32),
            pltpu.VMEM((2 * odd, 2, lines, width // 2), f32),
            pltpu.VMEM((sections, 2, piece, width), f32),
            pltpu.VMEM((wave_rows, sections, 2, lines, shard), f32),
            dma((steps,)),
            dma((steps,)),
            dma((3,)),
            dma((2,)),
            dma((1 + layers,)),
            dma((layers,)),
            dma((layers,)),
            dma((layers,)),
            dma((layers,)),
            dma((layers,)),
            dma((1,)),
        ],
        compiler_params=pltpu.CompilerParams(
            collective_id=0, has_side_effects=True, vmem_limit_bytes=60 * 1024 * 1024
        ),
    )(object_slices[0], probe_spec, measured, ramp_y, ramp_x, *tables)
    return result[None]


def fused_fits(sections, rows, waves, layers, width):
    if rows % waves or layers != sections or layers % 2:
        return False
    group = sections * rows // waves
    if width % group or width % rows or group % sections:
        return False
    lines, shard = width // group, width // rows
    if 2 * lines != 128 or shard != 2 * lines or width % 1024:
        return False
    return waves == 2 and sections == 4 and rows == 8


def solution(mesh):
    placed = (P("section", None, "row", None), P(None, "row", None), P(), P(None, "row", None))

    def build(body):
        return jax.shard_map(
            body,
            mesh=mesh,
            in_specs=placed,
            out_specs=P("section", None, "row", None),
            check_vma=False,
        )

    def run(object_slices, probe_spec, offsets, measured):
        fits = fused_fits(
            mesh.shape["section"], mesh.shape["row"], offsets.shape[0],
            object_slices.shape[0], object_slices.shape[3],
        )
        body = fused_shards if fits else shards
        return build(body)(object_slices, probe_spec, offsets, measured)

    return run
```
